256 devices in a mesh: span: 16 (over x_hi, z), seq: 16 (over x_lo, y, core).
Axes of the slice: x: 4 (x_hi: 2, x_lo: 2; x = x_hi * 2 + x_lo), y: 4, z: 8, core: 2. Of those that a mesh axis runs over, the one named last changes fastest.
Arguments:
- queries: bfloat16 [16, 2048, 4096], P('span', 'seq')
- keys: bfloat16 [16, 2048, 4096], P('span', 'seq')
- values: bfloat16 [16, 2048, 4096], P('span', 'seq'), may hold values from -6 to 6
- audio: bfloat16 [16, 1024, 1024], P('span', 'seq'), may hold values from -6 to 6
- audio_wk: bfloat16 [1024, 4096], P(None, 'seq'), may hold values from -0.1875 to 0.1875
- audio_wv: bfloat16 [1024, 4096], P(None, 'seq'), may hold values from -0.1875 to 0.1875
- frame_ids: int32 [16, 2048], P('span'), may hold values from 0 to 15, never falling along the last dimension, each value on 1 to 256 neighbouring positions
- windows: int32 [16, 16, 2], P('span'), may hold values from 0 to 1024, as said below
- video_start: int32 [16], P('span'), may hold values from 0 to 1, as said below
Outputs:
- attended: bfloat16 [16, 2048, 4096], P('span', 'seq')
The draws below stay inside these ranges and needn't reach their ends.
Inputs may be any that keep to these rules, and one draw needn't show every extreme that they name: windows[c, f] = (start, end) with 1 <= end - start <= 128; in every span frame 0's window is [0, 128) and the last frame's ends at 1024. video_start[0] = 1, and at least one of the spans 1 to 15 begins a new video.
All inputs are finite; a program needn't handle non-finite values.
Results may differ from the reference program's by a relative error of at most 0.0072.
Values may be sent and summed in bfloat16 or wider, within the bound.
A program may use at most 64 MiB of HBM per device.

```python
import math
import jax
import jax.numpy as jnp
import numpy as np
from jax import lax

HEADS = 32
HD = 128
AUD_W = 1024
SPANS = 16
SPAN_TOK = 2048
FRAMES = 16
FMOST = 256
AUD = 1024
WMAX = 128


def shared_keys(key):
    base = jax.random.normal(jax.random.fold_in(key, 7), (SPANS, SPAN_TOK, HEADS * HD), jnp.float32)
    base = jnp.clip(base, -4.0, 4.0)
    return base


def draw_keys(key, part):
    return shared_keys(key).astype(jnp.bfloat16)


def draw_queries(key, part):
    fresh = jax.random.normal(jax.random.fold_in(key, 13), (SPANS, SPAN_TOK, HEADS * HD), jnp.float32)
    fresh = jnp.clip(fresh, -4.0, 4.0)
    return fresh.astype(jnp.bfloat16)


def draw_windows(key, part):
    length = jax.random.randint(jax.random.fold_in(key, 3), (SPANS, FRAMES), 1, WMAX + 1)
    length = length.at[:, 0].set(WMAX)
    start = jax.random.randint(jax.random.fold_in(key, 5), (SPANS, FRAMES), 0, AUD - length + 1)
    start = start.at[:, 0].set(0)
    start = start.at[:, -1].set(AUD - length[:, -1])
    return jnp.stack([start, start + length], axis=-1).astype(jnp.int32)


def draw_video_start(key, part):
    positions = jnp.arange(SPANS, dtype=jnp.int32)
    coins = jax.random.randint(jax.random.fold_in(key, 29), (SPANS,), 0, 4)
    chosen = jax.random.randint(jax.random.fold_in(key, 23), (), 1, SPANS)
    marks = jnp.logical_or(coins == 0, positions == chosen)
    marks = jnp.logical_or(marks, positions == 0)
    return marks.astype(jnp.int32)


def shard_levels(stream_key, extent, pieces, smallest, high):
    def one(position, blocks):
        heights = jax.random.uniform(jax.random.fold_in(jax.random.fold_in(stream_key, 6), position), (blocks,), jnp.float32, smallest / len(pieces), high / len(pieces))
        return jnp.repeat(jnp.exp(heights), extent[position] // blocks).reshape((-1,) + (1,) * (len(extent) - position - 1))

    gain = one(*pieces[0])
    for cut in pieces[1:]:
        gain = gain * one(*cut)
    return gain


def split_up(number_of, total, reach, lean):
    loads = [(1 << 20) // math.isqrt(standing ** lean) + 1 for standing in range(2, number_of + 1)]
    spare, given = total - reach - (number_of - 1), [1] * (number_of - 1)
    while spare > 0:
        movable = [i for i in range(number_of - 1) if given[i] < reach]
        mass, budget = sum([loads[i] for i in movable]), spare
        for i in movable:
            addition = min(reach - given[i], max(1, budget * loads[i] // mass), spare)
            given[i] = given[i] + addition
            spare = spare - addition
    return np.array([reach] + given)


def uneven(rng, number_of, total, most, slope):
    if number_of == 2:
        one = jax.random.randint(rng, (), max(1, total - most), min(most, total - 1) + 1)
        return jnp.stack([one, total - one])
    tallies = jnp.asarray(split_up(number_of, total, most, slope), jnp.int32)
    couples = (number_of - 1) // 2
    giver, sink = tallies[1:1 + 2 * couples:2], tallies[2:2 + 2 * couples:2]
    slack = jnp.minimum(giver - 1, most - sink)
    passed = jax.random.randint(jax.random.fold_in(rng, 1), (couples,), 0, 1 << 20) % (slack + 1)
    tallies = tallies.at[1:1 + 2 * couples:2].set(giver - passed).at[2:2 + 2 * couples:2].set(sink + passed)
    return tallies[jax.random.permutation(jax.random.fold_in(rng, 2), number_of)]


def gaussian(stream_key, shape, scale, most, shards=(), kind=jnp.bfloat16):
    drawn = jax.random.normal(stream_key, shape, jnp.float32) * scale
    if len(shards) > 0:
        drawn = shard_levels(stream_key, shape, shards, -0.22, 0.18) * drawn
    return jnp.clip(drawn, min=-most, max=most).astype(kind)


def setup_inputs(seed: int = 0) -> dict:
    seeds = jax.random.split(jax.random.key(seed), 10)
    return {
        "queries": draw_queries(jax.random.fold_in(seeds[9], 71), 0),
        "keys": draw_keys(jax.random.fold_in(seeds[9], 71), 0),
        "values": gaussian(seeds[2], (SPANS, SPAN_TOK, HEADS * HD), 1.0, 6.0, ((0, 16), (1, 16))),
        "audio": gaussian(seeds[3], (SPANS, AUD, AUD_W), 1.0, 6.0, ((0, 16), (1, 16))),
        "audio_wk": gaussian(seeds[4], (AUD_W, HEADS * HD), AUD_W ** -0.5, 0.1875, ((1, 16),)),
        "audio_wv": gaussian(seeds[5], (AUD_W, HEADS * HD), AUD_W ** -0.5, 0.1875, ((1, 16),)),
        "frame_ids": jax.vmap(lambda own: jnp.searchsorted(jnp.cumsum(uneven(own, FRAMES, SPAN_TOK, FMOST, 1)), jnp.arange(SPAN_TOK), side="right"))(jax.random.split(seeds[6], SPANS)).reshape((SPANS, SPAN_TOK)).astype(jnp.int32),
        "windows": draw_windows(jax.random.fold_in(seeds[9], 71), 0),
        "video_start": draw_video_start(jax.random.fold_in(seeds[9], 71), 0),
    }


def attend(query, key_rows, value_rows, allowed, scale):
    scores = jnp.dot(query, key_rows.T, preferred_element_type=jnp.float32) * scale
    scores = jnp.where(allowed, scores, -1e30)
    top = jnp.max(scores, axis=-1, keepdims=True)
    weights = jnp.exp(scores - top)
    den = jnp.sum(weights, axis=-1, keepdims=True)
    numer = jnp.dot(weights.astype(jnp.bfloat16), value_rows, preferred_element_type=jnp.float32)
    return numer / den


def reference(queries, keys, values, audio, audio_wk, audio_wv, frame_ids, windows, video_start):
    scale = HD ** -0.5

    def one_span(index):
        prior = jnp.maximum(index - 1, 0).astype(jnp.int32)
        has_prev = jnp.logical_and(index > 0, video_start[index] == 0)
        frames = frame_ids[index]
        table = windows[index]
        lower = table[frames, 0]
        upper = table[frames, 1]
        own = frames[None, :] <= frames[:, None]
        before = jnp.broadcast_to(has_prev, (SPAN_TOK, SPAN_TOK))
        self_mask = jnp.concatenate([before, own], axis=1)
        positions = jnp.arange(AUD, dtype=jnp.int32)
        audio_mask = jnp.logical_and(positions[None, :] >= lower[:, None], positions[None, :] < upper[:, None])
        audio_keys = jnp.dot(audio[index], audio_wk, preferred_element_type=jnp.float32).astype(jnp.bfloat16)
        audio_vals = jnp.dot(audio[index], audio_wv, preferred_element_type=jnp.float32).astype(jnp.bfloat16)
        query_rows = queries[index]
        all_keys = jnp.concatenate([keys[prior], keys[index]], axis=0)
        all_vals = jnp.concatenate([values[prior], values[index]], axis=0)

        def one_head(head):
            start = (head * HD).astype(jnp.int32)

            def columns(array):
                return lax.dynamic_slice_in_dim(array, start, HD, 1)

            qh = columns(query_rows)
            self_out = attend(qh, columns(all_keys), columns(all_vals), self_mask, scale)
            audio_out = attend(qh, columns(audio_keys), columns(audio_vals), audio_mask, scale)
            return (self_out + audio_out).astype(jnp.bfloat16)

        heads_out = lax.map(one_head, jnp.arange(HEADS, dtype=jnp.int32))
        return jnp.transpose(heads_out, (1, 0, 2)).reshape(SPAN_TOK, HEADS * HD)

    return lax.map(one_span, jnp.arange(SPANS, dtype=jnp.int32))
```

```python
import jax
import jax.numpy as jnp
from jax import lax
from jax.sharding import PartitionSpec as P

HEADS = 32
HD = 128


def shifted(value, axis, steps):
    count = lax.axis_size(axis)
    leading, last = (max(0, -steps), min(count, count - steps))
    return lax.ppermute(value, axis, [(source, source + steps) for source in range(leading, last)])


def attend(query, key_rows, value_rows, allowed, scale):
    scores = jnp.einsum("qhd,khd->hqk", query, key_rows, preferred_element_type=jnp.float32) * scale
    scores = jnp.where(allowed[None, :, :], scores, -1e30)
    top = jnp.max(scores, axis=-1, keepdims=True)
    weights = jnp.exp(scores - top)
    den = jnp.sum(weights, axis=-1, keepdims=True)
    numer = jnp.einsum(
        "hqk,khd->qhd", weights.astype(jnp.bfloat16), value_rows, preferred_element_type=jnp.float32
    )
    return numer / jnp.transpose(den, (1, 0, 2))


def local(queries, keys, values, audio, audio_wk, audio_wv, frame_ids, windows, video_start):
    tok_rows = queries.shape[1]
    scale = HD ** (-0.5)
    q_local = queries.reshape(tok_rows, HEADS, HD)
    k_local = keys.reshape(tok_rows, HEADS, HD)
    v_local = values.reshape(tok_rows, HEADS, HD)
    k_heads, v_heads, q_heads = (
        lax.all_to_all(k_local, "seq", split_axis=1, concat_axis=0, tiled=True),
        lax.all_to_all(v_local, "seq", split_axis=1, concat_axis=0, tiled=True),
        lax.all_to_all(q_local, "seq", split_axis=1, concat_axis=0, tiled=True),
    )
    prev_kh, prev_vh = shifted((k_heads, v_heads), "span", 1)
    span_rows = q_heads.shape[0]
    head_count = q_heads.shape[1]
    joint_w = jnp.concatenate([audio_wk, audio_wv], axis=1)
    projected = jnp.dot(
        lax.all_gather(audio, "seq", axis=1, tiled=True)[0],
        joint_w,
        preferred_element_type=jnp.float32,
    ).astype(jnp.bfloat16)[None][0]
    aud_rows = projected.shape[0]
    audio_keys = projected[:, : head_count * HD].reshape(aud_rows, head_count, HD)
    audio_vals = projected[:, head_count * HD :].reshape(aud_rows, head_count, HD)
    has_prev = jnp.logical_and(lax.axis_index("span") > 0, video_start[0] == 0)
    frames = frame_ids[0]
    table = windows[0]
    onehot = frames[:, None] == jnp.arange(table.shape[0], dtype=jnp.int32)[None, :]
    lower = jnp.sum(jnp.where(onehot, table[None, :, 0], 0), axis=1)
    upper = jnp.sum(jnp.where(onehot, table[None, :, 1], 0), axis=1)
    all_keys = jnp.concatenate([prev_kh, k_heads], axis=0)
    all_vals = jnp.concatenate([prev_vh, v_heads], axis=0)
    positions = jnp.arange(aud_rows, dtype=jnp.int32)
    block = min(512, span_rows)

    def one_block(index):
        begin = index * block
        q_block = lax.dynamic_slice_in_dim(q_heads, begin, block, 0)
        f_block = lax.dynamic_slice_in_dim(frames, begin, block, 0)
        lo_block = lax.dynamic_slice_in_dim(lower, begin, block, 0)
        hi_block = lax.dynamic_slice_in_dim(upper, begin, block, 0)
        own = frames[None, :] <= f_block[:, None]
        before = jnp.broadcast_to(has_prev, (block, span_rows))
        self_mask = jnp.concatenate([before, own], axis=1)
        audio_mask = jnp.logical_and(
            positions[None, :] >= lo_block[:, None], positions[None, :] < hi_block[:, None]
        )
        self_out = attend(q_block, all_keys, all_vals, self_mask, scale)
        audio_out = attend(q_block, audio_keys, audio_vals, audio_mask, scale)
        return (self_out + audio_out).astype(jnp.bfloat16)

    blocks = lax.map(one_block, jnp.arange(span_rows // block, dtype=jnp.int32))
    mixed = blocks.reshape(span_rows, head_count, HD)
    back = lax.all_to_all(mixed, "seq", split_axis=0, concat_axis=1, tiled=True)
    return back.reshape(1, tok_rows, HEADS * HD)


def solution(mesh):
    placed = (
        P("span", "seq", None),
        P("span", "seq", None),
        P("span", "seq", None),
        P("span", "seq", None),
        P(None, "seq"),
        P(None, "seq"),
        P("span", None),
        P("span", None, None),
        P("span"),
    )
    return jax.shard_map(
        local, mesh=mesh, in_specs=placed, out_specs=P("span", "seq", None), check_vma=False
    )
```

```python
import functools

import jax
import jax.numpy as jnp
from jax import lax
from jax.experimental import pallas as pl
from jax.experimental.pallas import tpu as pltpu
from jax.sharding import PartitionSpec as P

HEADS = 32
HD = 128
TQ = 256
TK = 256
TA = 128
NEG = -1e30


def _attn_kernel(hp_ref, ncur_ref, alo_ref, ahi_ref,
                 q_ref, kc_ref, vc_ref, kp_ref, vp_ref, ka_ref, va_ref, meta_ref,
                 o_ref, sp_ref, sc_ref, sa_ref, *, scale):
    i = pl.program_id(1)
    has_prev = hp_ref[0] > 0
    ncur = ncur_ref[i]
    alo = alo_ref[i]
    ahi = ahi_ref[i]
    q = q_ref[...]
    kend = meta_ref[:, 0:1]
    lower = meta_ref[:, 1:2]
    upper = meta_ref[:, 2:3]
    tq = q.shape[0]
    nprev = kp_ref.shape[0] // TK
    dims = (((1,), (1,)), ((), ()))

    def scores(k):
        return lax.dot_general(q, k, dims, preferred_element_type=jnp.float32) * scale

    m0 = jnp.full((tq, 1), NEG, jnp.float32)

    def prev_max(c, m):
        at = pl.multiple_of(c * TK, TK)
        s = scores(kp_ref[pl.ds(at, TK), :])
        sp_ref[:, pl.ds(at, TK)] = s
        return jnp.maximum(m, jnp.max(s, axis=1, keepdims=True))

    m = lax.cond(has_prev, lambda mm: lax.fori_loop(0, nprev, prev_max, mm), lambda mm: mm, m0)

    def cur_max(c, m):
        at = pl.multiple_of(c * TK, TK)
        s = scores(kc_ref[pl.ds(at, TK), :])
        col = at + lax.broadcasted_iota(jnp.int32, s.shape, 1)
        s = jnp.where(col < kend, s, NEG)
        sc_ref[:, pl.ds(at, TK)] = s
        return jnp.maximum(m, jnp.max(s, axis=1, keepdims=True))

    m = lax.fori_loop(0, ncur, cur_max, m)

    l0 = jnp.zeros((tq, 1), jnp.float32)
    a0 = jnp.zeros((tq, HD), jnp.float32)

    def prev_sum(c, carry):
        l, acc = carry
        at = pl.multiple_of(c * TK, TK)
        p = jnp.exp(sp_ref[:, pl.ds(at, TK)] - m)
        l = l + jnp.sum(p, axis=1, keepdims=True)
        acc = acc + jnp.dot(p.astype(jnp.bfloat16), vp_ref[pl.ds(at, TK), :],
                            preferred_element_type=jnp.float32)
        return l, acc

    carry = lax.cond(has_prev, lambda cr: lax.fori_loop(0, nprev, prev_sum, cr), lambda cr: cr, (l0, a0))

    def cur_sum(c, carry):
        l, acc = carry
        at = pl.multiple_of(c * TK, TK)
        p = jnp.exp(sc_ref[:, pl.ds(at, TK)] - m)
        l = l + jnp.sum(p, axis=1, keepdims=True)
        acc = acc + jnp.dot(p.astype(jnp.bfloat16), vc_ref[pl.ds(at, TK), :],
                            preferred_element_type=jnp.float32)
        return l, acc

    l, acc = lax.fori_loop(0, ncur, cur_sum, carry)
    self_out = acc / l

    def aud_max(c, m):
        at = pl.multiple_of(c * TA, TA)
        s = scores(ka_ref[pl.ds(at, TA), :])
        pos = at + lax.broadcasted_iota(jnp.int32, s.shape, 1)
        s = jnp.where(jnp.logical_and(pos >= lower, pos < upper), s, NEG)
        sa_ref[:, pl.ds(at, TA)] = s
        return jnp.maximum(m, jnp.max(s, axis=1, keepdims=True))

    ma = lax.fori_loop(alo, ahi, aud_max, m0)

    def aud_sum(c, carry):
        l, acc = carry
        at = pl.multiple_of(c * TA, TA)
        p = jnp.exp(sa_ref[:, pl.ds(at, TA)] - ma)
        l = l + jnp.sum(p, axis=1, keepdims=True)
        acc = acc + jnp.dot(p.astype(jnp.bfloat16), va_ref[pl.ds(at, TA), :],
                            preferred_element_type=jnp.float32)
        return l, acc

    la, acca = lax.fori_loop(alo, ahi, aud_sum, (l0, a0))
    aud_out = acca / la
    o_ref[...] = (self_out + aud_out).astype(o_ref.dtype)


def fused_attention(q2, kc2, vc2, kp2, vp2, aud2, frames, table, has_prev):
    tokens, width = q2.shape
    heads = width // HD
    aud_rows = aud2.shape[0]
    nq = tokens // TQ
    scale = HD ** (-0.5)
    nf = table.shape[0]
    onehot = frames[:, None] == jnp.arange(nf, dtype=jnp.int32)[None, :]
    counts = jnp.sum(onehot.astype(jnp.int32), axis=0)
    cum = jnp.cumsum(counts)
    kend = jnp.sum(jnp.where(onehot, cum[None, :], 0), axis=1)
    lower = jnp.sum(jnp.where(onehot, table[None, :, 0], 0), axis=1)
    upper = jnp.sum(jnp.where(onehot, table[None, :, 1], 0), axis=1)
    meta = jnp.stack([kend, lower, upper], axis=1).astype(jnp.int32)
    ncur = (kend.reshape(nq, TQ)[:, -1] + TK - 1) // TK
    alo = jnp.min(lower.reshape(nq, TQ), axis=1) // TA
    ahi = (jnp.max(upper.reshape(nq, TQ), axis=1) + TA - 1) // TA
    hp = has_prev.astype(jnp.int32).reshape(1)

    full_k = pl.BlockSpec((tokens, HD), lambda h, i, *_: (0, h))
    full_a_k = pl.BlockSpec((aud_rows, HD), lambda h, i, *_: (0, h))
    full_a_v = pl.BlockSpec((aud_rows, HD), lambda h, i, *_: (0, heads + h))
    grid_spec = pltpu.PrefetchScalarGridSpec(
        num_scalar_prefetch=4,
        grid=(heads, nq),
        in_specs=[
            pl.BlockSpec((TQ, HD), lambda h, i, *_: (i, h)),
            full_k, full_k, full_k, full_k,
            full_a_k, full_a_v,
            pl.BlockSpec((TQ, 3), lambda h, i, *_: (i, 0)),
        ],
        out_specs=pl.BlockSpec((TQ, HD), lambda h, i, *_: (i, h)),
        scratch_shapes=[
            pltpu.VMEM((TQ, kp2.shape[0]), jnp.float32),
            pltpu.VMEM((TQ, tokens), jnp.float32),
            pltpu.VMEM((TQ, aud_rows), jnp.float32),
        ],
    )
    kv_rows = tokens + kp2.shape[0]
    flops = 4 * heads * tokens * HD * (kv_rows + aud_rows)
    cost = pl.CostEstimate(flops=flops, transcendentals=heads * tokens * (kv_rows + aud_rows),
                           bytes_accessed=2 * (5 * tokens * width + aud2.size))
    return pl.pallas_call(
        functools.partial(_attn_kernel, scale=scale),
        grid_spec=grid_spec,
        out_shape=jax.ShapeDtypeStruct((tokens, width), jnp.bfloat16),
        compiler_params=pltpu.CompilerParams(dimension_semantics=("arbitrary", "arbitrary")),
        cost_estimate=cost,
    )(hp, ncur, alo, ahi, q2, kc2, vc2, kp2, vp2, aud2, aud2, meta)


def shifted(value, axis, steps):
    count = lax.axis_size(axis)
    leading, last = (max(0, -steps), min(count, count - steps))
    return lax.ppermute(value, axis, [(source, source + steps) for source in range(leading, last)])


def local(queries, keys, values, audio, audio_wk, audio_wv, frame_ids, windows, video_start):
    tok_rows = queries.shape[1]
    groups = lax.axis_size("seq")
    width = HEADS * HD // groups

    def to_heads(x):
        x = x.reshape(tok_rows, groups, width)
        x = lax.all_to_all(x, "seq", split_axis=1, concat_axis=0, tiled=True)
        return x.reshape(tok_rows * groups, width)

    k2 = to_heads(keys)
    v2 = to_heads(values)
    q2 = to_heads(queries)
    kp2, vp2 = shifted((k2, v2), "span", 1)
    joint_w = jnp.concatenate([audio_wk, audio_wv], axis=1)
    aud2 = jnp.dot(
        lax.all_gather(audio, "seq", axis=1, tiled=True)[0],
        joint_w,
        preferred_element_type=jnp.float32,
    ).astype(jnp.bfloat16)
    has_prev = jnp.logical_and(lax.axis_index("span") > 0, video_start[0] == 0)
    out2 = fused_attention(q2, k2, v2, kp2, vp2, aud2, frame_ids[0], windows[0], has_prev)
    out3 = out2.reshape(tok_rows * groups, 1, width)
    back = lax.all_to_all(out3, "seq", split_axis=0, concat_axis=1, tiled=True)
    return back.reshape(1, tok_rows, HEADS * HD)


def solution(mesh):
    placed = (
        P("span", "seq", None),
        P("span", "seq", None),
        P("span", "seq", None),
        P("span", "seq", None),
        P(None, "seq"),
        P(None, "seq"),
        P("span", None),
        P("span", None, None),
        P("span"),
    )
    return jax.shard_map(
        local, mesh=mesh, in_specs=placed, out_specs=P("span", "seq", None), check_vma=False
    )
```

```python
import jax
import jax.numpy as jnp
from jax import lax
from jax.sharding import PartitionSpec as P

HEADS = 32
SEQ = ("chip", "core")
HD = 128


def shifted(value, axis, steps):
    count = lax.axis_size(axis)
    leading, last = (max(0, -steps), min(count, count - steps))
    return lax.ppermute(value, axis, [(source, source + steps) for source in range(leading, last)])


def attend(query, key_rows, value_rows, allowed, scale):
    scores = jnp.einsum("qhd,khd->hqk", query, key_rows, preferred_element_type=jnp.float32) * scale
    scores = jnp.where(allowed[None, :, :], scores, -1e30)
    top = jnp.max(scores, axis=-1, keepdims=True)
    weights = jnp.exp(scores - top)
    den = jnp.sum(weights, axis=-1, keepdims=True)
    numer = jnp.einsum(
        "hqk,khd->qhd", weights.astype(jnp.bfloat16), value_rows, preferred_element_type=jnp.float32
    )
    return numer / jnp.transpose(den, (1, 0, 2))


def local(queries, keys, values, audio, audio_wk, audio_wv, frame_ids, windows, video_start):
    tok_rows = queries.shape[1]
    scale = HD ** (-0.5)
    q_local = queries.reshape(tok_rows, HEADS, HD)
    k_local = keys.reshape(tok_rows, HEADS, HD)
    v_local = values.reshape(tok_rows, HEADS, HD)
    k_heads, v_heads, q_heads = (
        lax.all_to_all(k_local, SEQ, split_axis=1, concat_axis=0, tiled=True),
        lax.all_to_all(v_local, SEQ, split_axis=1, concat_axis=0, tiled=True),
        lax.all_to_all(q_local, SEQ, split_axis=1, concat_axis=0, tiled=True),
    )
    prev_kh, prev_vh = shifted((k_heads, v_heads), "span", 1)
    span_rows = q_heads.shape[0]
    head_count = q_heads.shape[1]
    joint_w = jnp.concatenate([audio_wk, audio_wv], axis=1)
    own = lax.all_gather(audio[0], "chip", axis=0, tiled=True)
    gathered = lax.all_gather(own, "core", axis=0, tiled=True)
    projected = jnp.dot(
        gathered,
        joint_w,
        preferred_element_type=jnp.float32,
    ).astype(jnp.bfloat16)[None][0]
    aud_rows = projected.shape[0]
    audio_keys = projected[:, : head_count * HD].reshape(aud_rows, head_count, HD)
    audio_vals = projected[:, head_count * HD :].reshape(aud_rows, head_count, HD)
    has_prev = jnp.logical_and(lax.axis_index("span") > 0, video_start[0] == 0)
    frames = frame_ids[0]
    table = windows[0]
    onehot = frames[:, None] == jnp.arange(table.shape[0], dtype=jnp.int32)[None, :]
    lower = jnp.sum(jnp.where(onehot, table[None, :, 0], 0), axis=1)
    upper = jnp.sum(jnp.where(onehot, table[None, :, 1], 0), axis=1)
    all_keys = jnp.concatenate([prev_kh, k_heads], axis=0)
    all_vals = jnp.concatenate([prev_vh, v_heads], axis=0)
    cores = lax.axis_size("core")
    chips = lax.axis_size("chip")
    piece = aud_rows // (cores * chips)
    order = jnp.arange(aud_rows, dtype=jnp.int32)
    held_core, held_chip, row = order // (chips * piece), (order // piece) % chips, order % piece
    positions = (held_chip * cores + held_core) * piece + row
    block = min(512, span_rows)

    def one_block(index):
        begin = index * block
        q_block = lax.dynamic_slice_in_dim(q_heads, begin, block, 0)
        f_block = lax.dynamic_slice_in_dim(frames, begin, block, 0)
        lo_block = lax.dynamic_slice_in_dim(lower, begin, block, 0)
        hi_block = lax.dynamic_slice_in_dim(upper, begin, block, 0)
        own = frames[None, :] <= f_block[:, None]
        before = jnp.broadcast_to(has_prev, (block, span_rows))
        self_mask = jnp.concatenate([before, own], axis=1)
        audio_mask = jnp.logical_and(
            positions[None, :] >= lo_block[:, None], positions[None, :] < hi_block[:, None]
        )
        self_out = attend(q_block, all_keys, all_vals, self_mask, scale)
        audio_out = attend(q_block, audio_keys, audio_vals, audio_mask, scale)
        return (self_out + audio_out).astype(jnp.bfloat16)

    blocks = lax.map(one_block, jnp.arange(span_rows // block, dtype=jnp.int32))
    mixed = blocks.reshape(span_rows, head_count, HD)
    back = lax.all_to_all(mixed, SEQ, split_axis=0, concat_axis=1, tiled=True)
    return back.reshape(1, tok_rows, HEADS * HD)


def solution(mesh):
    placed = (
        P("span", SEQ, None),
        P("span", SEQ, None),
        P("span", SEQ, None),
        P("span", SEQ, None),
        P(None, SEQ),
        P(None, SEQ),
        P("span", None),
        P("span", None, None),
        P("span"),
    )
    span, seq = mesh.devices.shape
    split = jax.sharding.Mesh(mesh.devices.reshape(span, seq // 2, 2), ("span", "chip", "core"))
    return jax.shard_map(
        local, mesh=split, in_specs=placed, out_specs=P("span", SEQ, None), check_vma=False
    )
```

```python
import jax
import jax.numpy as jnp
from jax import lax
from jax.sharding import PartitionSpec as P

HEADS = 32
SEQ = ("chip", "core")
HD = 128


def shifted(value, axis, steps):
    count = lax.axis_size(axis)
    leading, last = (max(0, -steps), min(count, count - steps))
    return lax.ppermute(value, axis, [(source, source + steps) for source in range(leading, last)])


def attend(query, key_rows, value_rows, allowed, scale):
    scores = jnp.einsum("qhd,khd->hqk", query, key_rows, preferred_element_type=jnp.float32) * scale
    scores = jnp.where(allowed[None, :, :], scores, -1e30)
    top = jnp.max(scores, axis=-1, keepdims=True)
    weights = jnp.exp(scores - top)
    den = jnp.sum(weights, axis=-1, keepdims=True)
    numer = jnp.einsum(
        "hqk,khd->qhd", weights.astype(jnp.bfloat16), value_rows, preferred_element_type=jnp.float32
    )
    return numer / jnp.transpose(den, (1, 0, 2))


def local(queries, keys, values, audio, audio_wk, audio_wv, frame_ids, windows, video_start):
    tok_rows = queries.shape[1]
    scale = HD ** (-0.5)
    q_local = queries.reshape(tok_rows, HEADS, HD)
    k_local = keys.reshape(tok_rows, HEADS, HD)
    v_local = values.reshape(tok_rows, HEADS, HD)
    k_heads, v_heads, q_heads = (
        lax.all_to_all(k_local, SEQ, split_axis=1, concat_axis=0, tiled=True),
        lax.all_to_all(v_local, SEQ, split_axis=1, concat_axis=0, tiled=True),
        lax.all_to_all(q_local, SEQ, split_axis=1, concat_axis=0, tiled=True),
    )
    prev_kh, prev_vh = shifted((k_heads, v_heads), "span", 1)
    span_rows = q_heads.shape[0]
    head_count = q_heads.shape[1]
    has_prev = jnp.logical_and(lax.axis_index("span") > 0, video_start[0] == 0)
    frames = frame_ids[0]
    table = windows[0]
    onehot = frames[:, None] == jnp.arange(table.shape[0], dtype=jnp.int32)[None, :]
    lower = jnp.sum(jnp.where(onehot, table[None, :, 0], 0), axis=1)
    upper = jnp.sum(jnp.where(onehot, table[None, :, 1], 0), axis=1)
    all_keys = jnp.concatenate([prev_kh, k_heads], axis=0)
    all_vals = jnp.concatenate([prev_vh, v_heads], axis=0)
    block = min(512, span_rows)

    def self_block(index):
        begin = index * block
        q_block = lax.dynamic_slice_in_dim(q_heads, begin, block, 0)
        f_block = lax.dynamic_slice_in_dim(frames, begin, block, 0)
        own = frames[None, :] <= f_block[:, None]
        before = jnp.broadcast_to(has_prev, (block, span_rows))
        self_mask = jnp.concatenate([before, own], axis=1)
        return attend(q_block, all_keys, all_vals, self_mask, scale)

    self_out = lax.map(self_block, jnp.arange(span_rows // block, dtype=jnp.int32))

    audio_late = lax.optimization_barrier((audio, q_heads, k_heads, v_heads))[0]
    joint_w = jnp.concatenate([audio_wk, audio_wv], axis=1)
    gathered = lax.all_gather(audio_late[0], SEQ, axis=0, tiled=True)
    projected = jnp.dot(
        gathered,
        joint_w,
        preferred_element_type=jnp.float32,
    ).astype(jnp.bfloat16)
    aud_rows = projected.shape[0]
    audio_keys = projected[:, : head_count * HD].reshape(aud_rows, head_count, HD)
    audio_vals = projected[:, head_count * HD :].reshape(aud_rows, head_count, HD)
    positions = jnp.arange(aud_rows, dtype=jnp.int32)

    def audio_block(index):
        begin = index * block
        q_block = lax.dynamic_slice_in_dim(q_heads, begin, block, 0)
        lo_block = lax.dynamic_slice_in_dim(lower, begin, block, 0)
        hi_block = lax.dynamic_slice_in_dim(upper, begin, block, 0)
        audio_mask = jnp.logical_and(
            positions[None, :] >= lo_block[:, None], positions[None, :] < hi_block[:, None]
        )
        audio_out = attend(q_block, audio_keys, audio_vals, audio_mask, scale)
        return (self_out[index] + audio_out).astype(jnp.bfloat16)

    blocks = lax.map(audio_block, jnp.arange(span_rows // block, dtype=jnp.int32))
    mixed = blocks.reshape(span_rows, head_count, HD)
    back = lax.all_to_all(mixed, SEQ, split_axis=0, concat_axis=1, tiled=True)
    return back.reshape(1, tok_rows, HEADS * HD)


def solution(mesh):
    placed = (
        P("span", SEQ, None),
        P("span", SEQ, None),
        P("span", SEQ, None),
        P("span", SEQ, None),
        P(None, SEQ),
        P(None, SEQ),
        P("span", None),
        P("span", None, None),
        P("span"),
    )
    span, seq = mesh.devices.shape
    split = jax.sharding.Mesh(mesh.devices.reshape(span, seq // 2, 2), ("span", "chip", "core"))
    return jax.shard_map(
        local, mesh=split, in_specs=placed, out_specs=P("span", SEQ, None), check_vma=False
    )
```

```python
import jax
import jax.numpy as jnp
from jax import lax
from jax.sharding import PartitionSpec as P

HEADS = 32
SEQ = ("chip", "core")
HD = 128


def shifted(value, axis, steps):
    count = lax.axis_size(axis)
    leading, last = (max(0, -steps), min(count, count - steps))
    return lax.ppermute(value, axis, [(source, source + steps) for source in range(leading, last)])


def attend(query, key_rows, value_rows, allowed, scale):
    scores = jnp.einsum("qhd,khd->hqk", query, key_rows, preferred_element_type=jnp.float32) * scale
    scores = jnp.where(allowed[None, :, :], scores, -1e30)
    top = jnp.max(scores, axis=-1, keepdims=True)
    weights = jnp.exp(scores - top)
    den = jnp.sum(weights, axis=-1, keepdims=True)
    numer = jnp.einsum(
        "hqk,khd->qhd", weights.astype(jnp.bfloat16), value_rows, preferred_element_type=jnp.float32
    )
    return numer / jnp.transpose(den, (1, 0, 2))


def local(queries, keys, values, audio, audio_wk, audio_wv, frame_ids, windows, video_start):
    tok_rows = queries.shape[1]
    scale = HD ** (-0.5)
    q_local = queries.reshape(tok_rows, HEADS, HD)
    k_local = keys.reshape(tok_rows, HEADS, HD)
    v_local = values.reshape(tok_rows, HEADS, HD)
    k_heads, v_heads, q_heads = (
        lax.all_to_all(k_local, SEQ, split_axis=1, concat_axis=0, tiled=True),
        lax.all_to_all(v_local, SEQ, split_axis=1, concat_axis=0, tiled=True),
        lax.all_to_all(q_local, SEQ, split_axis=1, concat_axis=0, tiled=True),
    )
    k_late, v_late = lax.optimization_barrier((k_heads, v_heads, q_heads))[:2]
    prev_kh, prev_vh = shifted((k_late, v_late), "span", 1)
    span_rows = q_heads.shape[0]
    head_count = q_heads.shape[1]
    joint_w = jnp.concatenate([audio_wk, audio_wv], axis=1)
    own = lax.all_gather(audio[0], "chip", axis=0, tiled=True)
    gathered = lax.all_gather(own, "core", axis=0, tiled=True)
    projected = jnp.dot(
        gathered,
        joint_w,
        preferred_element_type=jnp.float32,
    ).astype(jnp.bfloat16)[None][0]
    aud_rows = projected.shape[0]
    audio_keys = projected[:, : head_count * HD].reshape(aud_rows, head_count, HD)
    audio_vals = projected[:, head_count * HD :].reshape(aud_rows, head_count, HD)
    has_prev = jnp.logical_and(lax.axis_index("span") > 0, video_start[0] == 0)
    frames = frame_ids[0]
    table = windows[0]
    onehot = frames[:, None] == jnp.arange(table.shape[0], dtype=jnp.int32)[None, :]
    lower = jnp.sum(jnp.where(onehot, table[None, :, 0], 0), axis=1)
    upper = jnp.sum(jnp.where(onehot, table[None, :, 1], 0), axis=1)
    all_keys = jnp.concatenate([prev_kh, k_heads], axis=0)
    all_vals = jnp.concatenate([prev_vh, v_heads], axis=0)
    cores = lax.axis_size("core")
    chips = lax.axis_size("chip")
    piece = aud_rows // (cores * chips)
    order = jnp.arange(aud_rows, dtype=jnp.int32)
    held_core, held_chip, row = order // (chips * piece), (order // piece) % chips, order % piece
    positions = (held_chip * cores + held_core) * piece + row
    block = min(512, span_rows)

    def one_block(index):
        begin = index * block
        q_block = lax.dynamic_slice_in_dim(q_heads, begin, block, 0)
        f_block = lax.dynamic_slice_in_dim(frames, begin, block, 0)
        lo_block = lax.dynamic_slice_in_dim(lower, begin, block, 0)
        hi_block = lax.dynamic_slice_in_dim(upper, begin, block, 0)
        own = frames[None, :] <= f_block[:, None]
        before = jnp.broadcast_to(has_prev, (block, span_rows))
        self_mask = jnp.concatenate([before, own], axis=1)
        audio_mask = jnp.logical_and(
            positions[None, :] >= lo_block[:, None], positions[None, :] < hi_block[:, None]
        )
        self_out = attend(q_block, all_keys, all_vals, self_mask, scale)
        audio_out = attend(q_block, audio_keys, audio_vals, audio_mask, scale)
        return (self_out + audio_out).astype(jnp.bfloat16)

    blocks = lax.map(one_block, jnp.arange(span_rows // block, dtype=jnp.int32))
    mixed = blocks.reshape(span_rows, head_count, HD)
    back = lax.all_to_all(mixed, SEQ, split_axis=0, concat_axis=1, tiled=True)
    return back.reshape(1, tok_rows, HEADS * HD)


def solution(mesh):
    placed = (
        P("span", SEQ, None),
        P("span", SEQ, None),
        P("span", SEQ, None),
        P("span", SEQ, None),
        P(None, SEQ),
        P(None, SEQ),
        P("span", None),
        P("span", None, None),
        P("span"),
    )
    span, seq = mesh.devices.shape
    split = jax.sharding.Mesh(mesh.devices.reshape(span, seq // 2, 2), ("span", "chip", "core"))
    return jax.shard_map(
        local, mesh=split, in_specs=placed, out_specs=P("span", SEQ, None), check_vma=False
    )
```

```python
import jax
import jax.numpy as jnp
from jax import lax
from jax.sharding import PartitionSpec as P

HEADS = 32
SEQ = ("chip", "core")
HD = 128


def shifted(value, axis, steps):
    count = lax.axis_size(axis)
    leading, last = (max(0, -steps), min(count, count - steps))
    return lax.ppermute(value, axis, [(source, source + steps) for source in range(leading, last)])


def attend(query, key_rows, value_rows, allowed, scale):
    scores = jnp.einsum("qhd,khd->hqk", query, key_rows, preferred_element_type=jnp.float32) * scale
    scores = jnp.where(allowed[None, :, :], scores, -1e30)
    top = jnp.max(scores, axis=-1, keepdims=True)
    weights = jnp.exp(scores - top)
    den = jnp.sum(weights, axis=-1, keepdims=True)
    numer = jnp.einsum(
        "hqk,khd->qhd", weights.astype(jnp.bfloat16), value_rows, preferred_element_type=jnp.float32
    )
    return numer / jnp.transpose(den, (1, 0, 2))


def local(queries, keys, values, audio, audio_wk, audio_wv, frame_ids, windows, video_start):
    tok_rows = queries.shape[1]
    scale = HD ** (-0.5)
    q_local = queries.reshape(tok_rows, HEADS, HD)
    k_local = keys.reshape(tok_rows, HEADS, HD)
    v_local = values.reshape(tok_rows, HEADS, HD)
    k_heads, v_heads, q_heads = (
        lax.all_to_all(k_local, SEQ, split_axis=1, concat_axis=0, tiled=True),
        lax.all_to_all(v_local, SEQ, split_axis=1, concat_axis=0, tiled=True),
        lax.all_to_all(q_local, SEQ, split_axis=1, concat_axis=0, tiled=True),
    )
    k_late, v_late, audio_late = lax.optimization_barrier((k_heads, v_heads, audio, q_heads))[:3]
    prev_kh, prev_vh = shifted((k_late, v_late), "span", 1)
    span_rows = q_heads.shape[0]
    head_count = q_heads.shape[1]
    joint_w = jnp.concatenate([audio_wk, audio_wv], axis=1)
    gathered = lax.all_gather(audio_late[0], SEQ, axis=0, tiled=True)
    projected = jnp.dot(
        gathered,
        joint_w,
        preferred_element_type=jnp.float32,
    ).astype(jnp.bfloat16)[None][0]
    aud_rows = projected.shape[0]
    audio_keys = projected[:, : head_count * HD].reshape(aud_rows, head_count, HD)
    audio_vals = projected[:, head_count * HD :].reshape(aud_rows, head_count, HD)
    has_prev = jnp.logical_and(lax.axis_index("span") > 0, video_start[0] == 0)
    frames = frame_ids[0]
    table = windows[0]
    onehot = frames[:, None] == jnp.arange(table.shape[0], dtype=jnp.int32)[None, :]
    lower = jnp.sum(jnp.where(onehot, table[None, :, 0], 0), axis=1)
    upper = jnp.sum(jnp.where(onehot, table[None, :, 1], 0), axis=1)
    all_keys = jnp.concatenate([prev_kh, k_heads], axis=0)
    all_vals = jnp.concatenate([prev_vh, v_heads], axis=0)
    positions = jnp.arange(aud_rows, dtype=jnp.int32)
    block = min(512, span_rows)

    def one_block(index):
        begin = index * block
        q_block = lax.dynamic_slice_in_dim(q_heads, begin, block, 0)
        f_block = lax.dynamic_slice_in_dim(frames, begin, block, 0)
        lo_block = lax.dynamic_slice_in_dim(lower, begin, block, 0)
        hi_block = lax.dynamic_slice_in_dim(upper, begin, block, 0)
        own = frames[None, :] <= f_block[:, None]
        before = jnp.broadcast_to(has_prev, (block, span_rows))
        self_mask = jnp.concatenate([before, own], axis=1)
        audio_mask = jnp.logical_and(
            positions[None, :] >= lo_block[:, None], positions[None, :] < hi_block[:, None]
        )
        self_out = attend(q_block, all_keys, all_vals, self_mask, scale)
        audio_out = attend(q_block, audio_keys, audio_vals, audio_mask, scale)
        return (self_out + audio_out).astype(jnp.bfloat16)

    blocks = lax.map(one_block, jnp.arange(span_rows // block, dtype=jnp.int32))
    mixed = blocks.reshape(span_rows, head_count, HD)
    back = lax.all_to_all(mixed, SEQ, split_axis=0, concat_axis=1, tiled=True)
    return back.reshape(1, tok_rows, HEADS * HD)


def solution(mesh):
    placed = (
        P("span", SEQ, None),
        P("span", SEQ, None),
        P("span", SEQ, None),
        P("span", SEQ, None),
        P(None, SEQ),
        P(None, SEQ),
        P("span", None),
        P("span", None, None),
        P("span"),
    )
    span, seq = mesh.devices.shape
    split = jax.sharding.Mesh(mesh.devices.reshape(span, seq // 2, 2), ("span", "chip", "core"))
    return jax.shard_map(
        local, mesh=split, in_specs=placed, out_specs=P("span", SEQ, None), check_vma=False
    )
```

```python
import jax
import jax.numpy as jnp
from jax import lax
from jax.sharding import PartitionSpec as P

HEADS = 32
FMOST = 256
SEQ = ("chip", "core")
HD = 128


def shifted(value, axis, steps):
    count = lax.axis_size(axis)
    leading, last = (max(0, -steps), min(count, count - steps))
    return lax.ppermute(value, axis, [(source, source + steps) for source in range(leading, last)])


def attend(query, key_rows, value_rows, allowed, scale):
    scores = jnp.einsum("qhd,khd->hqk", query, key_rows, preferred_element_type=jnp.float32) * scale
    scores = jnp.where(allowed[None, :, :], scores, -1e30)
    top = jnp.max(scores, axis=-1, keepdims=True)
    weights = jnp.exp(scores - top)
    den = jnp.sum(weights, axis=-1, keepdims=True)
    numer = jnp.einsum(
        "hqk,khd->qhd", weights.astype(jnp.bfloat16), value_rows, preferred_element_type=jnp.float32
    )
    return numer / jnp.transpose(den, (1, 0, 2))


def local(queries, keys, values, audio, audio_wk, audio_wv, frame_ids, windows, video_start):
    tok_rows = queries.shape[1]
    scale = HD ** (-0.5)
    q_local = queries.reshape(tok_rows, HEADS, HD)
    k_local = keys.reshape(tok_rows, HEADS, HD)
    v_local = values.reshape(tok_rows, HEADS, HD)
    k_heads, v_heads, q_heads = (
        lax.all_to_all(k_local, SEQ, split_axis=1, concat_axis=0, tiled=True),
        lax.all_to_all(v_local, SEQ, split_axis=1, concat_axis=0, tiled=True),
        lax.all_to_all(q_local, SEQ, split_axis=1, concat_axis=0, tiled=True),
    )
    prev_kh, prev_vh = shifted((k_heads, v_heads), "span", 1)
    span_rows = q_heads.shape[0]
    head_count = q_heads.shape[1]
    joint_w = jnp.concatenate([audio_wk, audio_wv], axis=1)
    own = lax.all_gather(audio[0], "chip", axis=0, tiled=True)
    gathered = lax.all_gather(own, "core", axis=0, tiled=True)
    projected = jnp.dot(
        gathered,
        joint_w,
        preferred_element_type=jnp.float32,
    ).astype(jnp.bfloat16)[None][0]
    aud_rows = projected.shape[0]
    audio_keys = projected[:, : head_count * HD].reshape(aud_rows, head_count, HD)
    audio_vals = projected[:, head_count * HD :].reshape(aud_rows, head_count, HD)
    has_prev = jnp.logical_and(lax.axis_index("span") > 0, video_start[0] == 0)
    frames = frame_ids[0]
    table = windows[0]
    onehot = frames[:, None] == jnp.arange(table.shape[0], dtype=jnp.int32)[None, :]
    lower = jnp.sum(jnp.where(onehot, table[None, :, 0], 0), axis=1)
    upper = jnp.sum(jnp.where(onehot, table[None, :, 1], 0), axis=1)
    cores = lax.axis_size("core")
    chips = lax.axis_size("chip")
    piece = aud_rows // (cores * chips)
    order = jnp.arange(aud_rows, dtype=jnp.int32)
    held_core, held_chip, row = order // (chips * piece), (order // piece) % chips, order % piece
    positions = (held_chip * cores + held_core) * piece + row
    block = min(512, span_rows)
    prev_rows = prev_kh.shape[0]
    pieces = []
    for index in range(span_rows // block):
        begin = index * block
        extent = min(span_rows, begin + block + FMOST)
        q_block = q_heads[begin : begin + block]
        if pieces:
            q_block = lax.optimization_barrier((q_block, pieces[-1]))[0]
        f_block = frames[begin : begin + block]
        lo_block = lower[begin : begin + block]
        hi_block = upper[begin : begin + block]
        own = frames[None, :extent] <= f_block[:, None]
        before = jnp.broadcast_to(has_prev, (block, prev_rows))
        self_mask = jnp.concatenate([before, own], axis=1)
        audio_mask = jnp.logical_and(
            positions[None, :] >= lo_block[:, None], positions[None, :] < hi_block[:, None]
        )
        keys_used = jnp.concatenate([prev_kh, k_heads[:extent]], axis=0)
        vals_used = jnp.concatenate([prev_vh, v_heads[:extent]], axis=0)
        self_out = attend(q_block, keys_used, vals_used, self_mask, scale)
        audio_out = attend(q_block, audio_keys, audio_vals, audio_mask, scale)
        pieces.append((self_out + audio_out).astype(jnp.bfloat16))
    blocks = jnp.concatenate(pieces, axis=0)
    mixed = blocks.reshape(span_rows, head_count, HD)
    back = lax.all_to_all(mixed, SEQ, split_axis=0, concat_axis=1, tiled=True)
    return back.reshape(1, tok_rows, HEADS * HD)


def solution(mesh):
    placed = (
        P("span", SEQ, None),
        P("span", SEQ, None),
        P("span", SEQ, None),
        P("span", SEQ, None),
        P(None, SEQ),
        P(None, SEQ),
        P("span", None),
        P("span", None, None),
        P("span"),
    )
    span, seq = mesh.devices.shape
    split = jax.sharding.Mesh(mesh.devices.reshape(span, seq // 2, 2), ("span", "chip", "core"))
    return jax.shard_map(
        local, mesh=split, in_specs=placed, out_specs=P("span", SEQ, None), check_vma=False
    )
```

```python
import jax
import jax.numpy as jnp
from jax import lax
from jax.sharding import PartitionSpec as P

HEADS = 32
SEQ = ("chip", "core")
HD = 128


def shifted(value, axis, steps):
    count = lax.axis_size(axis)
    leading, last = (max(0, -steps), min(count, count - steps))
    return lax.ppermute(value, axis, [(source, source + steps) for source in range(leading, last)])


def attend(query, key_rows, value_rows, allowed, scale):
    scores = jnp.einsum("qhd,khd->hqk", query, key_rows, preferred_element_type=jnp.float32) * scale
    scores = jnp.where(allowed[None, :, :], scores, -1e30)
    top = jnp.max(scores, axis=-1, keepdims=True)
    weights = jnp.exp(scores - top)
    den = jnp.sum(weights, axis=-1, keepdims=True)
    numer = jnp.einsum(
        "hqk,khd->qhd", weights.astype(jnp.bfloat16), value_rows, preferred_element_type=jnp.float32
    )
    return numer / jnp.transpose(den, (1, 0, 2))


def local(queries, keys, values, audio, audio_wk, audio_wv, frame_ids, windows, video_start):
    tok_rows = queries.shape[1]
    scale = HD ** (-0.5)
    q_local = queries.reshape(tok_rows, HEADS, HD)
    k_local = keys.reshape(tok_rows, HEADS, HD)
    v_local = values.reshape(tok_rows, HEADS, HD)
    k_heads, v_heads, q_heads = (
        lax.all_to_all(k_local, SEQ, split_axis=1, concat_axis=0, tiled=True),
        lax.all_to_all(v_local, SEQ, split_axis=1, concat_axis=0, tiled=True),
        lax.all_to_all(q_local, SEQ, split_axis=1, concat_axis=0, tiled=True),
    )
    prev_kh, prev_vh = shifted((k_heads, v_heads), "span", 1)
    span_rows = q_heads.shape[0]
    head_count = q_heads.shape[1]
    joint_w = jnp.concatenate([audio_wk, audio_wv], axis=1)
    own = lax.all_gather(audio[0], "chip", axis=0, tiled=True)
    gathered = lax.all_gather(own, "core", axis=0, tiled=True)
    projected = jnp.dot(
        gathered,
        joint_w,
        preferred_element_type=jnp.float32,
    ).astype(jnp.bfloat16)[None][0]
    aud_rows = projected.shape[0]
    audio_keys = projected[:, : head_count * HD].reshape(aud_rows, head_count, HD)
    audio_vals = projected[:, head_count * HD :].reshape(aud_rows, head_count, HD)
    has_prev = jnp.logical_and(lax.axis_index("span") > 0, video_start[0] == 0)
    frames = frame_ids[0]
    table = windows[0]
    onehot = frames[:, None] == jnp.arange(table.shape[0], dtype=jnp.int32)[None, :]
    lower = jnp.sum(jnp.where(onehot, table[None, :, 0], 0), axis=1)
    upper = jnp.sum(jnp.where(onehot, table[None, :, 1], 0), axis=1)
    all_keys = jnp.concatenate([prev_kh, k_heads], axis=0)
    all_vals = jnp.concatenate([prev_vh, v_heads], axis=0)
    cores = lax.axis_size("core")
    chips = lax.axis_size("chip")
    piece = aud_rows // (cores * chips)
    order = jnp.arange(aud_rows, dtype=jnp.int32)
    held_core, held_chip, row = order // (chips * piece), (order // piece) % chips, order % piece
    positions = (held_chip * cores + held_core) * piece + row
    block = min(512, span_rows)

    def one_block(index):
        begin = index * block
        q_block = lax.dynamic_slice_in_dim(q_heads, begin, block, 0)
        f_block = lax.dynamic_slice_in_dim(frames, begin, block, 0)
        lo_block = lax.dynamic_slice_in_dim(lower, begin, block, 0)
        hi_block = lax.dynamic_slice_in_dim(upper, begin, block, 0)
        own = frames[None, :] <= f_block[:, None]
        before = jnp.broadcast_to(has_prev, (block, span_rows))
        self_mask = jnp.concatenate([before, own], axis=1)
        audio_mask = jnp.logical_and(
            positions[None, :] >= lo_block[:, None], positions[None, :] < hi_block[:, None]
        )
        self_out = attend(q_block, all_keys, all_vals, self_mask, scale)
        audio_out = attend(q_block, audio_keys, audio_vals, audio_mask, scale)
        return (self_out + audio_out).astype(jnp.bfloat16).reshape(block, head_count * HD)

    blocks = lax.map(one_block, jnp.arange(span_rows // block, dtype=jnp.int32))
    mixed = blocks.reshape(span_rows, head_count * HD)
    back = lax.all_to_all(mixed, SEQ, split_axis=0, concat_axis=1, tiled=True)
    return back.reshape(1, tok_rows, HEADS * HD)


def solution(mesh):
    placed = (
        P("span", SEQ, None),
        P("span", SEQ, None),
        P("span", SEQ, None),
        P("span", SEQ, None),
        P(None, SEQ),
        P(None, SEQ),
        P("span", None),
        P("span", None, None),
        P("span"),
    )
    span, seq = mesh.devices.shape
    split = jax.sharding.Mesh(mesh.devices.reshape(span, seq // 2, 2), ("span", "chip", "core"))
    return jax.shard_map(
        local, mesh=split, in_specs=placed, out_specs=P("span", SEQ, None), check_vma=False
    )
```

```python
import jax
import jax.numpy as jnp
from jax import lax
from jax.sharding import PartitionSpec as P

HEADS = 32
SEQ = ("chip", "core")
HD = 128


def shifted(value, axis, steps):
    count = lax.axis_size(axis)
    leading, last = (max(0, -steps), min(count, count - steps))
    return lax.ppermute(value, axis, [(source, source + steps) for source in range(leading, last)])


def attend(query, key_rows, value_rows, allowed, scale):
    scores = jnp.einsum("qhd,khd->hqk", query, key_rows, preferred_element_type=jnp.float32) * scale
    scores = jnp.where(allowed[None, :, :], scores, -1e30)
    top = jnp.max(scores, axis=-1, keepdims=True)
    weights = jnp.exp(scores - top)
    den = jnp.sum(weights, axis=-1, keepdims=True)
    numer = jnp.einsum(
        "hqk,khd->qhd", weights.astype(jnp.bfloat16), value_rows, preferred_element_type=jnp.float32
    )
    return numer / jnp.transpose(den, (1, 0, 2))


def local(queries, keys, values, audio, audio_wk, audio_wv, frame_ids, windows, video_start):
    tok_rows = queries.shape[1]
    scale = HD ** (-0.5)
    q_local = queries.reshape(tok_rows, HEADS, HD)
    k_local = keys.reshape(tok_rows, HEADS, HD)
    v_local = values.reshape(tok_rows, HEADS, HD)
    k_heads, v_heads, q_heads = (
        lax.all_to_all(k_local, SEQ, split_axis=1, concat_axis=0, tiled=True),
        lax.all_to_all(v_local, SEQ, split_axis=1, concat_axis=0, tiled=True),
        lax.all_to_all(q_local, SEQ, split_axis=1, concat_axis=0, tiled=True),
    )
    prev_kh, prev_vh = shifted((k_heads, v_heads), "span", 1)
    span_rows = q_heads.shape[0]
    head_count = q_heads.shape[1]
    joint_w = jnp.concatenate([audio_wk, audio_wv], axis=1)
    own = lax.all_gather(audio[0], "chip", axis=0, tiled=True)
    gathered = lax.all_gather(own, "core", axis=0, tiled=True)
    projected = jnp.dot(
        gathered,
        joint_w,
        preferred_element_type=jnp.float32,
    ).astype(jnp.bfloat16)[None][0]
    aud_rows = projected.shape[0]
    audio_keys = projected[:, : head_count * HD].reshape(aud_rows, head_count, HD)
    audio_vals = projected[:, head_count * HD :].reshape(aud_rows, head_count, HD)
    has_prev = jnp.logical_and(lax.axis_index("span") > 0, video_start[0] == 0)
    frames = frame_ids[0]
    table = windows[0]
    onehot = frames[:, None] == jnp.arange(table.shape[0], dtype=jnp.int32)[None, :]
    lower = jnp.sum(jnp.where(onehot, table[None, :, 0], 0), axis=1)
    upper = jnp.sum(jnp.where(onehot, table[None, :, 1], 0), axis=1)
    all_keys = jnp.concatenate([prev_kh, k_heads], axis=0)
    all_vals = jnp.concatenate([prev_vh, v_heads], axis=0)
    cores = lax.axis_size("core")
    chips = lax.axis_size("chip")
    piece = aud_rows // (cores * chips)
    order = jnp.arange(aud_rows, dtype=jnp.int32)
    held_core, held_chip, row = order // (chips * piece), (order // piece) % chips, order % piece
    positions = (held_chip * cores + held_core) * piece + row
    block = min(1024, span_rows)
    groups = HEADS // head_count
    outs = []
    for g in range(head_count):
        q_g, k_g, v_g = q_heads[:, g : g + 1], all_keys[:, g : g + 1], all_vals[:, g : g + 1]
        ak_g, av_g = audio_keys[:, g : g + 1], audio_vals[:, g : g + 1]

        def one_block(index, q_g=q_g, k_g=k_g, v_g=v_g, ak_g=ak_g, av_g=av_g):
            begin = index * block
            q_block = lax.dynamic_slice_in_dim(q_g, begin, block, 0)
            f_block = lax.dynamic_slice_in_dim(frames, begin, block, 0)
            lo_block = lax.dynamic_slice_in_dim(lower, begin, block, 0)
            hi_block = lax.dynamic_slice_in_dim(upper, begin, block, 0)
            own = frames[None, :] <= f_block[:, None]
            before = jnp.broadcast_to(has_prev, (block, span_rows))
            self_mask = jnp.concatenate([before, own], axis=1)
            audio_mask = jnp.logical_and(
                positions[None, :] >= lo_block[:, None], positions[None, :] < hi_block[:, None]
            )
            self_out = attend(q_block, k_g, v_g, self_mask, scale)
            audio_out = attend(q_block, ak_g, av_g, audio_mask, scale)
            return (self_out + audio_out).astype(jnp.bfloat16).reshape(block, HD)

        blocks = lax.map(one_block, jnp.arange(span_rows // block, dtype=jnp.int32))
        mixed = blocks.reshape(span_rows, HD)
        outs.append(lax.all_to_all(mixed, SEQ, split_axis=0, concat_axis=1, tiled=True).reshape(tok_rows, groups, 1, HD))
    back = jnp.concatenate(outs, axis=2)
    return back.reshape(1, tok_rows, HEADS * HD)


def solution(mesh):
    placed = (
        P("span", SEQ, None),
        P("span", SEQ, None),
        P("span", SEQ, None),
        P("span", SEQ, None),
        P(None, SEQ),
        P(None, SEQ),
        P("span", None),
        P("span", None, None),
        P("span"),
    )
    span, seq = mesh.devices.shape
    split = jax.sharding.Mesh(mesh.devices.reshape(span, seq // 2, 2), ("span", "chip", "core"))
    return jax.shard_map(
        local, mesh=split, in_specs=placed, out_specs=P("span", SEQ, None), check_vma=False
    )
```

```python
import jax
import jax.numpy as jnp
from jax import lax
from jax.sharding import PartitionSpec as P


HEADS = 32
SEQ = ("chip", "core")
HD = 128


def shifted(value, axis, steps):
    count = lax.axis_size(axis)
    leading, last = (max(0, -steps), min(count, count - steps))
    return lax.ppermute(value, axis, [(source, source + steps) for source in range(leading, last)])


def attend(query, key_rows, value_rows, allowed, scale):
    scores = jnp.einsum("qhd,khd->hqk", query, key_rows, preferred_element_type=jnp.float32) * scale
    scores = jnp.where(allowed[None, :, :], scores, -1e30)
    top = jnp.max(scores, axis=-1, keepdims=True)
    weights = jnp.exp(scores - top)
    den = jnp.sum(weights, axis=-1, keepdims=True)
    numer = jnp.einsum(
        "hqk,khd->qhd", weights.astype(jnp.bfloat16), value_rows, preferred_element_type=jnp.float32
    )
    return numer / jnp.transpose(den, (1, 0, 2))


def step(queries, keys, values, audio, audio_wk, audio_wv, frame_ids, windows, video_start):
    tok_rows = queries.shape[1]
    scale = HD ** (-0.5)
    q_local = queries.reshape(tok_rows, HEADS, HD)
    k_local = keys.reshape(tok_rows, HEADS, HD)
    v_local = values.reshape(tok_rows, HEADS, HD)
    k_heads, v_heads, q_heads = (
        lax.all_to_all(k_local, SEQ, split_axis=1, concat_axis=0, tiled=True),
        lax.all_to_all(v_local, SEQ, split_axis=1, concat_axis=0, tiled=True),
        lax.all_to_all(q_local, SEQ, split_axis=1, concat_axis=0, tiled=True),
    )
    span_rows = q_heads.shape[0]
    head_count = q_heads.shape[1]
    joint_w = jnp.concatenate([audio_wk, audio_wv], axis=1)
    own = lax.all_gather(audio[0], "chip", axis=0, tiled=True)
    gathered = lax.all_gather(own, "core", axis=0, tiled=True)
    projected = jnp.dot(
        gathered,
        joint_w,
        preferred_element_type=jnp.float32,
    ).astype(jnp.bfloat16)[None][0]
    aud_rows = projected.shape[0]
    audio_keys = projected[:, : head_count * HD].reshape(aud_rows, head_count, HD)
    audio_vals = projected[:, head_count * HD :].reshape(aud_rows, head_count, HD)
    has_prev = jnp.logical_and(lax.axis_index("span") > 0, video_start[0] == 0)
    frames = frame_ids[0]
    table = windows[0]
    onehot = frames[:, None] == jnp.arange(table.shape[0], dtype=jnp.int32)[None, :]
    lower = jnp.sum(jnp.where(onehot, table[None, :, 0], 0), axis=1)
    upper = jnp.sum(jnp.where(onehot, table[None, :, 1], 0), axis=1)
    cores = lax.axis_size("core")
    chips = lax.axis_size("chip")
    piece = aud_rows // (cores * chips)
    order = jnp.arange(aud_rows, dtype=jnp.int32)
    held_core, held_chip, row = order // (chips * piece), (order // piece) % chips, order % piece
    positions = (held_chip * cores + held_core) * piece + row
    block = min(1024, span_rows)
    groups = HEADS // head_count
    outs = []
    for g in range(head_count):
        cur_k, cur_v = k_heads[:, g : g + 1], v_heads[:, g : g + 1]
        prev_k, prev_v = shifted(jnp.stack([cur_k, cur_v]), "span", 1)
        q_g = q_heads[:, g : g + 1]
        k_g = jnp.concatenate([prev_k, cur_k], axis=0)
        v_g = jnp.concatenate([prev_v, cur_v], axis=0)
        ak_g, av_g = audio_keys[:, g : g + 1], audio_vals[:, g : g + 1]

        def one_block(index, q_g=q_g, k_g=k_g, v_g=v_g, ak_g=ak_g, av_g=av_g):
            begin = index * block
            q_block = lax.dynamic_slice_in_dim(q_g, begin, block, 0)
            f_block = lax.dynamic_slice_in_dim(frames, begin, block, 0)
            lo_block = lax.dynamic_slice_in_dim(lower, begin, block, 0)
            hi_block = lax.dynamic_slice_in_dim(upper, begin, block, 0)
            own = frames[None, :] <= f_block[:, None]
            before = jnp.broadcast_to(has_prev, (block, span_rows))
            self_mask = jnp.concatenate([before, own], axis=1)
            audio_mask = jnp.logical_and(
                positions[None, :] >= lo_block[:, None], positions[None, :] < hi_block[:, None]
            )
            self_out = attend(q_block, k_g, v_g, self_mask, scale)
            audio_out = attend(q_block, ak_g, av_g, audio_mask, scale)
            return (self_out + audio_out).astype(jnp.bfloat16).reshape(block, HD)

        blocks = lax.map(one_block, jnp.arange(span_rows // block, dtype=jnp.int32))
        mixed = blocks.reshape(span_rows, HD)
        outs.append(lax.all_to_all(mixed, SEQ, split_axis=0, concat_axis=1, tiled=True).reshape(tok_rows, groups, 1, HD))
    back = jnp.concatenate(outs, axis=2)
    return back.reshape(1, tok_rows, HEADS * HD)


def solution(mesh):
    placed = (
        P("span", SEQ, None),
        P("span", SEQ, None),
        P("span", SEQ, None),
        P("span", SEQ, None),
        P(None, SEQ),
        P(None, SEQ),
        P("span", None),
        P("span", None, None),
        P("span"),
    )
    span, seq = mesh.devices.shape
    split = jax.sharding.Mesh(mesh.devices.reshape(span, seq // 2, 2), ("span", "chip", "core"))
    return jax.shard_map(
        step, mesh=split, in_specs=placed, out_specs=P("span", SEQ, None), check_vma=False
    )
```
